32 devices in a mesh: seq: 8 (over y, x, core), slate: 4 (over z).
Axes of the slice: x: 2, y: 2, z: 4, core: 2. Of those that a mesh axis runs over, the one named last changes fastest.
Arguments:
- features: bfloat16 [4, 6144, 512], P('slate', 'seq'), may hold values from -6 to 6
- user_ids: int32 [4], P('slate'), may hold values from 0 to 1023
- labels: int32 [4, 6144], P('slate', 'seq'), may hold values from 0 to 4, as said below
- user_table: bfloat16 [1024, 512], replicated, may hold values from -3 to 3
- gain_in: float32 [512], replicated, may hold values from 0.5 to 1.5
- w_query: bfloat16 [512, 512], replicated, may hold values from -0.75 to 0.75
- w_key: bfloat16 [512, 512], replicated, may hold values from -0.75 to 0.75
- w_value: bfloat16 [512, 512], replicated, may hold values from -0.25 to 0.25
- w_out: bfloat16 [512, 512], replicated, may hold values from -0.25 to 0.25
- gain_out: float32 [512], replicated, may hold values from 0.5 to 1.5
- w_score: float32 [512], replicated, may hold values from -0.25 to 0.25
Outputs:
- mixed: bfloat16 [4, 6144, 512], P('slate', 'seq')
- scores: float32 [4, 6144], P('slate', 'seq')
- loss: float32 [], replicated
The draws below stay inside these ranges and needn't reach their ends.
Inputs may be any that keep to these rules, and one draw needn't show every extreme that they name: `labels`: relevance grades of the items.
All inputs are finite; a program needn't handle non-finite values.
Results may differ from the reference program's by a relative error of at most 0.0045.
Values may be sent and summed in bfloat16 or wider, within the bound.
No kernel may reach another device: no remote copies, remote signals or barrier semaphores. Data moves between devices by JAX's collectives and lax.ppermute only.
A program may use at most 192 MiB of HBM per device.

```python
import math
import jax
import jax.numpy as jnp
from jax import lax

D = 512
HEADS = 8
ITEM_DEV = 768
USERS = 1024
ITEMS = 6144
SLATES = 4


def draw_labels(key, part):
    position = jnp.arange(ITEMS, dtype=jnp.int32)
    upper = 2 + 4 * position // ITEMS
    upper = jnp.broadcast_to(upper[None, :], (SLATES, ITEMS))
    return jax.random.randint(jax.random.fold_in(key, 17), (SLATES, ITEMS), 0, upper, dtype=jnp.int32)


def plant(result, key, low, high):
    place = [jax.random.randint(jax.random.fold_in(key, axis), (), 0, length) for axis, length in enumerate(result.shape)]
    widest = result.shape.index(max(result.shape))
    next_to = place[:widest] + [(place[widest] + 1) % result.shape[widest]] + place[widest + 1:]
    return result.at[tuple(place)].set(low).at[tuple(next_to)].set(high)


def block_levels(key, dims, split, low, high):
    level, own = 1.0, jax.random.fold_in(key, 6)
    for dim, parts in split:
        heights = jnp.exp(jax.random.uniform(jax.random.fold_in(own, dim), (parts,), jnp.float32, low / len(split), high / len(split)))
        level = level * jnp.repeat(heights, dims[dim] // parts).reshape([-1 if axis == dim else 1 for axis in range(len(dims))])
    return level


def scatter_about(key, extent, deviation, reach, cuts=(), held_as=jnp.bfloat16):
    loudness = block_levels(key, extent, cuts, -0.22, 0.18) if cuts else 1.0
    entries = jax.random.normal(key, extent, jnp.float32) * deviation * loudness
    return jnp.minimum(jnp.maximum(entries, -reach), reach).astype(held_as)


def setup_inputs(seed: int = 0) -> dict:
    splits = jax.random.split(jax.random.key(seed), 12)
    features = scatter_about(splits[0], (SLATES, ITEMS, D), 1.0, 6.0, ((0, 4), (1, 8)))
    user_ids = plant(jax.random.randint(splits[1], (SLATES,), 0, USERS), jax.random.fold_in(splits[1], 1), 0, USERS - 1).astype(jnp.int32)
    labels = draw_labels(jax.random.fold_in(splits[11], 71), 0)
    user_table = scatter_about(splits[3], (USERS, D), 0.5, 3.0)
    gain_in = jnp.clip(1.0 + 0.1 * jax.random.normal(splits[4], (D,), jnp.float32), 0.5, 1.5)
    w_query = scatter_about(splits[5], (D, D), (D // 8) ** -0.5, 0.75)
    w_key = scatter_about(splits[6], (D, D), (D // 8) ** -0.5, 0.75)
    w_value = scatter_about(splits[7], (D, D), D ** -0.5, 0.25)
    w_out = scatter_about(splits[8], (D, D), D ** -0.5, 0.25)
    gain_out = jnp.clip(1.0 + 0.1 * jax.random.normal(splits[9], (D,), jnp.float32), 0.5, 1.5)
    w_score = scatter_about(splits[10], (D,), D ** -0.5, 0.25, (), jnp.float32)
    return dict(features=features, user_ids=user_ids, labels=labels, user_table=user_table, gain_in=gain_in, w_query=w_query, w_key=w_key, w_value=w_value, w_out=w_out, gain_out=gain_out, w_score=w_score)


soft_cap = 20.0
norm_eps = 1e-06

def rms_norm(inputs_row, gain_row):
    return inputs_row * lax.rsqrt(lax.optimization_barrier(jnp.mean(inputs_row * inputs_row, axis=-1, keepdims=True)) + norm_eps) * gain_row

def slate_pass(features, user_id, labels, user_table, gain_in, w_query, w_key, w_value, w_out, gain_out, w_score):
    item_rows = features.shape[0]
    model_width = features.shape[1]
    head_dim = model_width // HEADS
    score_scale = 1.0 / math.sqrt(head_dim)
    one_hot = (jnp.arange(user_table.shape[0], dtype=jnp.int32) == user_id).astype(jnp.bfloat16)[None, :]
    personal = jnp.dot(one_hot, user_table, preferred_element_type=jnp.float32)
    hidden = features.astype(jnp.float32) + personal
    normed = rms_norm(hidden, gain_in).astype(jnp.bfloat16)
    queries = jnp.dot(normed, w_query, preferred_element_type=jnp.float32).astype(jnp.bfloat16)
    keys_proj = jnp.dot(normed, w_key, preferred_element_type=jnp.float32).astype(jnp.bfloat16)
    values_proj = jnp.dot(normed, w_value, preferred_element_type=jnp.float32).astype(jnp.bfloat16)
    keys_all = keys_proj.reshape(item_rows, HEADS, head_dim).astype(jnp.float32)
    values_all = values_proj.reshape(item_rows, HEADS, head_dim).astype(jnp.float32)
    blocks = queries.reshape(item_rows // ITEM_DEV, ITEM_DEV, HEADS, head_dim)

    def attend(query_block):
        logits = jnp.einsum('qhd,khd->hqk', query_block.astype(jnp.float32), keys_all) * score_scale
        exp_scores = jnp.exp(soft_cap * jnp.tanh(logits / soft_cap))
        totals = lax.optimization_barrier(jnp.sum(exp_scores, axis=-1))
        rounded = lax.optimization_barrier(exp_scores.astype(jnp.bfloat16)).astype(jnp.float32)
        weighted = jnp.einsum('hqk,khd->qhd', rounded, values_all)
        return weighted / jnp.transpose(totals)[:, :, None]
    attended = lax.map(attend, blocks).reshape(item_rows, model_width).astype(jnp.bfloat16)
    mixed_sum = hidden + jnp.dot(attended, w_out, preferred_element_type=jnp.float32)
    out_normed = rms_norm(mixed_sum, gain_out)
    scored = lax.optimization_barrier(jnp.sum(out_normed * w_score, axis=-1))
    label_weight = jnp.exp(labels.astype(jnp.float32))
    partition = jnp.sum(jnp.exp(scored))
    slate_loss = jnp.log(partition / float(item_rows)) - jnp.sum(label_weight * scored) / jnp.sum(label_weight)
    return (mixed_sum.astype(jnp.bfloat16), scored, slate_loss)

def reference(features, user_ids, labels, user_table, gain_in, w_query, w_key, w_value, w_out, gain_out, w_score):

    def per_slate(inputs):
        return slate_pass(inputs[0], inputs[1], inputs[2], user_table, gain_in, w_query, w_key, w_value, w_out, gain_out, w_score)
    mixed, scores, losses = lax.map(per_slate, (features, user_ids, labels))
    return (mixed, scores, jnp.sum(losses))
```

```python
import math

import jax
import jax.numpy as jnp
from jax import lax
from jax.experimental import pallas as pl
from jax.experimental.pallas import tpu as pltpu
from jax.sharding import PartitionSpec as P

HEADS = 8
TILE = 256
BLOCK = 16

soft_cap = 20.0
norm_eps = 1e-06
bf16, f32 = jnp.bfloat16, jnp.float32

VMEM = pl.BlockSpec(memory_space=pltpu.VMEM)


def dot(lhs, rhs, contract):
    return lax.dot_general(lhs, rhs, ((contract[:1], contract[1:]), ((), ())), preferred_element_type=f32)


def user_row(ids_ref, table_ref):
    rows = table_ref[...].astype(f32)
    mine = lax.broadcasted_iota(jnp.int32, rows.shape, 0) == lax.rem(ids_ref[0], BLOCK)
    return jnp.sum(jnp.where(mine, rows, 0.0), axis=0, keepdims=True)


def norm_kernel(ids_ref, features_ref, table_ref, gain_ref, normed_ref):
    hidden = features_ref[...].astype(f32) + user_row(ids_ref, table_ref)
    scale = lax.rsqrt(jnp.mean(hidden * hidden, axis=-1, keepdims=True) + norm_eps)
    normed_ref[...] = (hidden * scale * gain_ref[...]).astype(bf16)


def normalise(user_ids, features, user_table, gain_in):
    rows, width = features.shape
    return pl.pallas_call(
        norm_kernel,
        name="normalise",
        grid_spec=pltpu.PrefetchScalarGridSpec(
            num_scalar_prefetch=1,
            grid=(rows // TILE,),
            in_specs=[
                pl.BlockSpec((TILE, width), lambda i, ids: (i, 0)),
                pl.BlockSpec((BLOCK, width), lambda i, ids: (ids[0] // BLOCK, 0)),
                pl.BlockSpec((1, width), lambda i, ids: (0, 0)),
            ],
            out_specs=pl.BlockSpec((TILE, width), lambda i, ids: (i, 0)),
        ),
        out_shape=jax.ShapeDtypeStruct((rows, width), bf16),
    )(user_ids, features, user_table, gain_in)


def attend(pieces, w_key, first=None, later=None, last=None):
    rows, width = pieces[0].shape
    queries = rows
    head_dim = width // HEADS
    held = head_dim + 16
    keys = rows * len(pieces)
    tiles = keys // TILE
    to_tanh = 1.0 / (math.sqrt(head_dim) * soft_cap)
    to_exp2 = soft_cap / math.log(2.0)

    def body(*refs):
        refs = list(refs)
        piece_refs = [refs.pop(0) for _ in pieces]
        wk_ref = refs.pop(0)
        if first:
            wq_ref, wv_ref = refs.pop(0), refs.pop(0)
        else:
            q_ref, wvt_ref, acc_in = refs.pop(0), refs.pop(0), refs.pop(0)
        if last:
            ids_ref, features_ref, table_ref, wout_ref, gain_ref, wscore_ref, labels_ref = (refs.pop(0) for _ in range(7))
            mixed_ref, scores_ref, sums_ref = (refs.pop(0) for _ in range(3))
        else:
            acc_ref = refs.pop(0)
            if first:
                q_ref, wvt_ref = refs.pop(0), refs.pop(0)
        x_ref, s0, s1, p0, p1, k_now, k_next, v_now, v_next, v_last = (refs.pop(0) for _ in range(10))
        if last:
            acc_ref, attended_ref = refs.pop(0), refs.pop(0)
        s_slots, p_slots = (s0, s1), (p0, p1)
        ones = jnp.ones((16, TILE), bf16)

        for i, piece in enumerate(piece_refs):
            x_ref[i * rows : (i + 1) * rows, :] = piece[...]
        if first:
            wvt_ref[...] = wv_ref[...].T
            zero = jnp.zeros((head_dim, queries), bf16)
            wqt = wq_ref[...].T
            for h in range(HEADS):
                q_head = dot(wqt[h * head_dim : (h + 1) * head_dim, :], piece_refs[0][...], (1, 1)).astype(bf16)
                q_ref[h] = jnp.concatenate([zero, q_head] if h % 2 else [q_head, zero], axis=0)
            acc_ref[...] = jnp.zeros_like(acc_ref)
        elif last:
            acc_ref[...] = acc_in[...]

        def project_keys(tile, half):
            x = x_ref[pl.ds(pl.multiple_of(tile * TILE, TILE), TILE), :]
            cols = slice(half * width // 2, (half + 1) * width // 2)
            k_next[:, cols] = dot(x, wk_ref[:, cols], (1, 0)).astype(bf16)

        def project_values(tile, half):
            x = x_ref[pl.ds(pl.multiple_of(tile * TILE, TILE), TILE), :]
            cols = slice(half * width // 2, (half + 1) * width // 2)
            v_next[cols, :] = dot(wvt_ref[cols, :], x, (1, 1)).astype(bf16)

        def score(k_ref, h, slot):
            pair = h // 2 * 2 * head_dim
            s_slots[slot][...] = dot(k_ref[:, pair : pair + 2 * head_dim], q_ref[h], (1, 0))

        def weigh(slot):
            capped = jnp.tanh(s_slots[slot][...] * to_tanh)
            p_slots[slot][...] = jnp.exp2(capped * to_exp2).astype(bf16)

        def add_values(values, h, slot):
            held_values = jnp.concatenate([values, ones], axis=0)
            acc_ref[h] += dot(held_values, p_slots[slot][...], (1, 0))

        def step():
            last_head = slice((HEADS - 1) * head_dim, HEADS * head_dim)
            v_last[...] = v_now[last_head, :]
            k_now[...] = k_next[...]
            v_now[...] = v_next[...]

        for half in range(2):
            project_keys(0, half)
            project_values(0, half)
        k_now[...] = k_next[...]
        v_now[...] = v_next[...]
        v_last[...] = jnp.zeros_like(v_last)
        p1[...] = jnp.zeros_like(p1)
        score(k_now, 0, 0)

        @pl.loop(0, tiles)
        def _(tile):
            following = jnp.minimum(tile + 1, tiles - 1)
            for h in range(HEADS):
                slot, other = h % 2, (h + 1) % 2
                if h + 1 < HEADS:
                    score(k_now, h + 1, other)
                else:
                    score(k_next, 0, other)
                weigh(slot)
                if h == 0:
                    add_values(v_last[...], HEADS - 1, other)
                else:
                    add_values(v_now[(h - 1) * head_dim : h * head_dim, :], h - 1, other)
                if h < 2:
                    project_keys(following, h)
                elif h < 4:
                    project_values(following, h - 2)
            step()

        add_values(v_last[...], HEADS - 1, 1)

        if last:
            for h in range(HEADS):
                head = slice(h * head_dim, (h + 1) * head_dim)
                attended_ref[head, :] = (acc_ref[h, :head_dim, :] / acc_ref[h, head_dim : head_dim + 1, :]).astype(bf16)
            personal = user_row(ids_ref, table_ref)
            exp_sum = weight_sum = product_sum = 0.0
            for i in range(queries // TILE):
                here = slice(i * TILE, (i + 1) * TILE)
                hidden = features_ref[here, :].astype(f32) + personal
                mixed = hidden + dot(attended_ref[:, here], wout_ref[...], (0, 0))
                mixed_ref[here, :] = mixed.astype(bf16)
                scale = lax.rsqrt(jnp.mean(mixed * mixed, axis=-1, keepdims=True) + norm_eps)
                scored = jnp.sum(mixed * scale * gain_ref[...] * wscore_ref[...], axis=-1, keepdims=True)
                line = jnp.broadcast_to(scored, (TILE, 128)).T[:1, :]
                scores_ref[:, here] = line
                weight = jnp.exp(labels_ref[:, here].astype(f32))
                exp_sum = exp_sum + jnp.sum(jnp.exp(line), axis=-1, keepdims=True)
                weight_sum = weight_sum + jnp.sum(weight, axis=-1, keepdims=True)
                product_sum = product_sum + jnp.sum(weight * line, axis=-1, keepdims=True)
            row = lax.broadcasted_iota(jnp.int32, sums_ref.shape, 0)
            sums_ref[...] = jnp.where(row == 0, exp_sum, jnp.where(row == 1, weight_sum, product_sum))

    tile_scratch = [
        pltpu.VMEM((keys, width), bf16),
        *[pltpu.VMEM((TILE, queries), f32)] * 2,
        *[pltpu.VMEM((TILE, queries), bf16)] * 2,
        *[pltpu.VMEM((TILE, width), bf16)] * 2,
        *[pltpu.VMEM((width, TILE), bf16)] * 2,
        pltpu.VMEM((head_dim, TILE), bf16),
    ]
    acc_shape = jax.ShapeDtypeStruct((HEADS, held, queries), f32)
    operands = [*pieces, w_key]
    specs = [VMEM] * len(operands)
    aliases = {}
    if first:
        operands += first
        specs += [VMEM] * 2
        outs = [acc_shape, jax.ShapeDtypeStruct((HEADS, 2 * head_dim, queries), bf16), jax.ShapeDtypeStruct((width, width), bf16)]
    else:
        operands += later
        specs += [VMEM] * 3
        outs = [acc_shape]
        aliases = {len(operands) - 1: 0}
    if last:
        user_ids, features, user_table, w_out, gain_out, w_score, labels = last
        operands += [user_ids, features, user_table, w_out, gain_out, w_score, labels]
        specs += [pl.BlockSpec(memory_space=pltpu.SMEM)] + [VMEM] * 6
        outs = [
            jax.ShapeDtypeStruct((queries, width), bf16),
            jax.ShapeDtypeStruct((1, queries), f32),
            jax.ShapeDtypeStruct((8, 128), f32),
        ]
        aliases = {}
        tile_scratch += [pltpu.VMEM(acc_shape.shape, f32), pltpu.VMEM((width, queries), bf16)]
    products = HEADS * keys * queries
    return pl.pallas_call(
        body,
        name="attend",
        in_specs=specs,
        out_specs=[VMEM] * len(outs),
        out_shape=outs,
        scratch_shapes=tile_scratch,
        input_output_aliases=aliases,
        compiler_params=pltpu.CompilerParams(vmem_limit_bytes=28 << 20),
        cost_estimate=pl.CostEstimate(flops=4 * head_dim * products, transcendentals=2 * products, bytes_accessed=8 << 20),
    )(*operands)


def exchange(value, axis, bit):
    size = lax.axis_size(axis)
    return lax.ppermute(value, axis, [(i, i ^ bit) for i in range(size)])


def total(value, axis):
    size = lax.axis_size(axis)
    if size & (size - 1):
        return lax.psum(value, axis)
    bit = 1
    while bit < size:
        value = value + exchange(value, axis, bit)
        bit *= 2
    return value


def shards(features, user_ids, labels, user_table, gain_in, w_query, w_key, w_value, w_out, gain_out, w_score):
    local_items = features[0]
    item_rows = local_items.shape[0]
    group = lax.axis_size("seq")
    slate_items = float(item_rows * group)
    normed = normalise(user_ids, local_items, user_table, gain_in[None])
    swap = lambda value: exchange(value, "seq", 1)

    partner = swap(normed)
    far = [exchange(normed, "seq", bit) for bit in range(2, group, 2)]
    passes = [[normed, partner]]
    for i in range(0, len(far), 2):
        near = far[i : i + 2]
        passes += [near, [swap(piece) for piece in near]]
    weighted, q_heads, w_value_t = attend(passes[0], w_key, first=[w_query, w_value])
    for pieces in passes[1:-1]:
        (weighted,) = attend(pieces, w_key, later=[q_heads, w_value_t, weighted])
    start = user_ids[0] // BLOCK * BLOCK
    user_rows = lax.dynamic_slice_in_dim(user_table, start, BLOCK, 0)
    mixed, scored, sums = attend(
        passes[-1],
        w_key,
        later=[q_heads, w_value_t, weighted],
        last=[user_ids, local_items, user_rows, w_out, gain_out[None], w_score[None], labels],
    )
    sums = total(sums[:3, :1], "seq")
    slate_loss = jnp.log(sums[0, 0] / slate_items) - sums[2, 0] / sums[1, 0]
    total_loss = total(slate_loss[None, None], "slate")
    return (mixed[None], scored, total_loss[0, 0])


def solution(mesh):
    return jax.shard_map(
        shards,
        mesh=mesh,
        in_specs=(
            P("slate", "seq", None),
            P("slate"),
            P("slate", "seq"),
            P(),
            P(),
            P(),
            P(),
            P(),
            P(),
            P(),
            P(),
        ),
        out_specs=(P("slate", "seq", None), P("slate", "seq"), P()),
        check_vma=False,
    )
```

```python
import math

import jax
import jax.numpy as jnp
from jax import lax
from jax.experimental import pallas as pl
from jax.experimental.pallas import tpu as pltpu
from jax.sharding import PartitionSpec as P

HEADS = 8
TILE = 256
BLOCK = 16

soft_cap = 20.0
norm_eps = 1e-06
bf16, f32 = jnp.bfloat16, jnp.float32

VMEM = pl.BlockSpec(memory_space=pltpu.VMEM)
HBM = pl.BlockSpec(memory_space=pltpu.HBM)


def dot(lhs, rhs, contract):
    return lax.dot_general(lhs, rhs, ((contract[:1], contract[1:]), ((), ())), preferred_element_type=f32)


def prepare(user_ids, features, user_table, gain_in, weights):
    rows, width = features.shape
    parts = rows // TILE

    def body(ids_ref, features_hbm, table_hbm, gain_hbm, *refs):
        weights_hbm, refs = refs[: len(weights)], refs[len(weights) :]
        normed_ref, personal_ref, refs = refs[0], refs[1], refs[2:]
        weight_refs, (features_ref, table_ref, gain_ref, sem) = refs[: len(weights)], refs[len(weights) :]
        start = pl.multiple_of(lax.div(ids_ref[0], BLOCK) * BLOCK, BLOCK)
        here = [slice(i * TILE, (i + 1) * TILE) for i in range(parts)]
        small = [
            pltpu.make_async_copy(table_hbm.at[pl.ds(start, BLOCK), :], table_ref, sem.at[0]),
            pltpu.make_async_copy(gain_hbm, gain_ref, sem.at[1]),
        ]
        items = [pltpu.make_async_copy(features_hbm.at[at, :], features_ref.at[at, :], sem.at[2 + i]) for i, at in enumerate(here)]
        large = [pltpu.make_async_copy(w, to, sem.at[2 + parts + i]) for i, (w, to) in enumerate(zip(weights_hbm, weight_refs))]
        for copy in small + items + large:
            copy.start()
        for copy in small:
            copy.wait()
        table = table_ref[...].astype(f32)
        mine = lax.broadcasted_iota(jnp.int32, table.shape, 0) == lax.rem(ids_ref[0], BLOCK)
        personal = jnp.sum(jnp.where(mine, table, 0.0), axis=0, keepdims=True)
        personal_ref[...] = jnp.broadcast_to(personal, personal_ref.shape)
        for copy, at in zip(items, here):
            copy.wait()
            hidden = features_ref[at, :].astype(f32) + personal
            scale = lax.rsqrt(jnp.mean(hidden * hidden, axis=-1, keepdims=True) + norm_eps)
            normed_ref[at, :] = (hidden * scale * gain_ref[...]).astype(bf16)
        for copy in large:
            copy.wait()

    outs = [jax.ShapeDtypeStruct((rows, width), bf16), jax.ShapeDtypeStruct((8, width), f32)]
    outs += [jax.ShapeDtypeStruct(w.shape, w.dtype) for w in weights]
    normed, personal, *held = pl.pallas_call(
        body,
        name="prepare",
        in_specs=[pl.BlockSpec(memory_space=pltpu.SMEM)] + [HBM] * (3 + len(weights)),
        out_specs=[VMEM] * len(outs),
        out_shape=outs,
        scratch_shapes=[
            pltpu.VMEM((rows, width), bf16),
            pltpu.VMEM((BLOCK, width), bf16),
            pltpu.VMEM((1, width), f32),
            pltpu.SemaphoreType.DMA((2 + parts + len(weights),)),
        ],
        compiler_params=pltpu.CompilerParams(vmem_limit_bytes=16 << 20),
        cost_estimate=pl.CostEstimate(flops=8 * rows * width, transcendentals=rows, bytes_accessed=4 << 20),
    )(user_ids, *(pltpu.with_memory_space_constraint(x, pltpu.HBM) for x in (features, user_table, gain_in, *weights)))
    return normed, personal, held


def project_queries(normed, w_query, w_value):
    rows, width = normed.shape
    head_dim = width // HEADS

    def body(x_ref, wq_ref, wv_ref, q_ref, wvt_ref):
        wvt_ref[...] = wv_ref[...].T
        zero = jnp.zeros((head_dim, rows), bf16)
        wqt = wq_ref[...].T
        for h in range(HEADS):
            q_head = dot(wqt[h * head_dim : (h + 1) * head_dim, :], x_ref[...], (1, 1)).astype(bf16)
            q_ref[h] = jnp.concatenate([zero, q_head] if h % 2 else [q_head, zero], axis=0)

    return pl.pallas_call(
        body,
        name="project_queries",
        in_specs=[VMEM] * 3,
        out_specs=[VMEM] * 2,
        out_shape=[jax.ShapeDtypeStruct((HEADS, 2 * head_dim, rows), bf16), jax.ShapeDtypeStruct((width, width), bf16)],
        compiler_params=pltpu.CompilerParams(vmem_limit_bytes=16 << 20),
        cost_estimate=pl.CostEstimate(flops=2 * rows * width * width, transcendentals=0, bytes_accessed=4 << 20),
    )(normed, w_query, w_value)


def attend(pieces, w_key, w_value_t, q_heads, weighted=None, last=None):
    rows, width = pieces[0].shape
    queries = rows
    head_dim = width // HEADS
    held = head_dim + 16
    keys = rows * len(pieces)
    tiles = keys // TILE
    to_tanh = 1.0 / (math.sqrt(head_dim) * soft_cap)
    to_exp2 = soft_cap / math.log(2.0)

    def body(*refs):
        refs = list(refs)
        piece_refs = [refs.pop(0) for _ in pieces]
        wk_ref, wvt_ref, q_ref = (refs.pop(0) for _ in range(3))
        if weighted is not None:
            acc_in = refs.pop(0)
        if last:
            personal_ref, features_ref, wout_ref, gain_ref, wscore_ref, labels_ref = (refs.pop(0) for _ in range(6))
            mixed_ref, scores_ref, sums_ref = (refs.pop(0) for _ in range(3))
        else:
            acc_ref = refs.pop(0)
        x_ref, s0, s1, p0, p1, k_now, k_next, v_now, v_next, v_last = (refs.pop(0) for _ in range(10))
        if last:
            acc_ref, attended_ref = refs.pop(0), refs.pop(0)
        s_slots, p_slots = (s0, s1), (p0, p1)
        ones = jnp.ones((16, TILE), bf16)

        for i, piece in enumerate(piece_refs):
            x_ref[i * rows : (i + 1) * rows, :] = piece[...]
        if weighted is None:
            acc_ref[...] = jnp.zeros_like(acc_ref)
        elif last:
            acc_ref[...] = acc_in[...]

        def project_keys(tile, half):
            x = x_ref[pl.ds(pl.multiple_of(tile * TILE, TILE), TILE), :]
            cols = slice(half * width // 2, (half + 1) * width // 2)
            k_next[:, cols] = dot(x, wk_ref[:, cols], (1, 0)).astype(bf16)

        def project_values(tile, half):
            x = x_ref[pl.ds(pl.multiple_of(tile * TILE, TILE), TILE), :]
            cols = slice(half * width // 2, (half + 1) * width // 2)
            v_next[cols, :] = dot(wvt_ref[cols, :], x, (1, 1)).astype(bf16)

        def score(k_ref, h, slot):
            pair = h // 2 * 2 * head_dim
            s_slots[slot][...] = dot(k_ref[:, pair : pair + 2 * head_dim], q_ref[h], (1, 0))

        def weigh(slot):
            capped = jnp.tanh(s_slots[slot][...] * to_tanh)
            p_slots[slot][...] = jnp.exp2(capped * to_exp2).astype(bf16)

        def add_values(values, h, slot):
            held_values = jnp.concatenate([values, ones], axis=0)
            acc_ref[h] += dot(held_values, p_slots[slot][...], (1, 0))

        def step():
            last_head = slice((HEADS - 1) * head_dim, HEADS * head_dim)
            v_last[...] = v_now[last_head, :]
            k_now[...] = k_next[...]
            v_now[...] = v_next[...]

        for half in range(2):
            project_keys(0, half)
            project_values(0, half)
        k_now[...] = k_next[...]
        v_now[...] = v_next[...]
        v_last[...] = jnp.zeros_like(v_last)
        p1[...] = jnp.zeros_like(p1)
        score(k_now, 0, 0)

        @pl.loop(0, tiles)
        def _(tile):
            following = jnp.minimum(tile + 1, tiles - 1)
            for h in range(HEADS):
                slot, other = h % 2, (h + 1) % 2
                if h + 1 < HEADS:
                    score(k_now, h + 1, other)
                else:
                    score(k_next, 0, other)
                weigh(slot)
                if h == 0:
                    add_values(v_last[...], HEADS - 1, other)
                else:
                    add_values(v_now[(h - 1) * head_dim : h * head_dim, :], h - 1, other)
                if h < 2:
                    project_keys(following, h)
                elif h < 4:
                    project_values(following, h - 2)
            step()

        add_values(v_last[...], HEADS - 1, 1)

        if last:
            for h in range(HEADS):
                head = slice(h * head_dim, (h + 1) * head_dim)
                attended_ref[head, :] = (acc_ref[h, :head_dim, :] / acc_ref[h, head_dim : head_dim + 1, :]).astype(bf16)
            personal = personal_ref[:1, :]
            exp_sum = weight_sum = product_sum = 0.0
            for i in range(queries // TILE):
                here = slice(i * TILE, (i + 1) * TILE)
                hidden = features_ref[here, :].astype(f32) + personal
                mixed = hidden + dot(attended_ref[:, here], wout_ref[...], (0, 0))
                mixed_ref[here, :] = mixed.astype(bf16)
                scale = lax.rsqrt(jnp.mean(mixed * mixed, axis=-1, keepdims=True) + norm_eps)
                scored = jnp.sum(mixed * scale * gain_ref[...] * wscore_ref[...], axis=-1, keepdims=True)
                line = jnp.broadcast_to(scored, (TILE, 128)).T[:1, :]
                scores_ref[:, here] = line
                weight = jnp.exp(labels_ref[:, here].astype(f32))
                exp_sum = exp_sum + jnp.sum(jnp.exp(line), axis=-1, keepdims=True)
                weight_sum = weight_sum + jnp.sum(weight, axis=-1, keepdims=True)
                product_sum = product_sum + jnp.sum(weight * line, axis=-1, keepdims=True)
            lane = lax.broadcasted_iota(jnp.int32, sums_ref.shape, 1)
            sums_ref[...] = jnp.where(lane == 0, exp_sum, jnp.where(lane == 1, weight_sum, product_sum))

    tile_scratch = [
        pltpu.VMEM((keys, width), bf16),
        *[pltpu.VMEM((TILE, queries), f32)] * 2,
        *[pltpu.VMEM((TILE, queries), bf16)] * 2,
        *[pltpu.VMEM((TILE, width), bf16)] * 2,
        *[pltpu.VMEM((width, TILE), bf16)] * 2,
        pltpu.VMEM((head_dim, TILE), bf16),
    ]
    acc_shape = jax.ShapeDtypeStruct((HEADS, held, queries), f32)
    operands = [*pieces, w_key, w_value_t, q_heads]
    aliases = {}
    outs = [acc_shape]
    if weighted is not None:
        operands += [weighted]
        aliases = {len(operands) - 1: 0}
    if last:
        operands += last
        outs = [
            jax.ShapeDtypeStruct((queries, width), bf16),
            jax.ShapeDtypeStruct((1, queries), f32),
            jax.ShapeDtypeStruct((8, 128), f32),
        ]
        aliases = {}
        tile_scratch += [pltpu.VMEM(acc_shape.shape, f32), pltpu.VMEM((width, queries), bf16)]
    products = HEADS * keys * queries
    return pl.pallas_call(
        body,
        name="attend",
        in_specs=[VMEM] * len(operands),
        out_specs=[VMEM] * len(outs),
        out_shape=outs,
        scratch_shapes=tile_scratch,
        input_output_aliases=aliases,
        compiler_params=pltpu.CompilerParams(vmem_limit_bytes=28 << 20),
        cost_estimate=pl.CostEstimate(flops=4 * head_dim * products, transcendentals=2 * products, bytes_accessed=8 << 20),
    )(*operands)


def exchange(value, axis, bit):
    size = lax.axis_size(axis)
    return lax.ppermute(value, axis, [(i, i ^ bit) for i in range(size)])


def after(values, event):
    return lax.optimization_barrier((values, event))


def shards(features, user_ids, labels, user_table, gain_in, w_query, w_key, w_value, w_out, gain_out, w_score):
    local_items = features[0]
    item_rows = local_items.shape[0]
    group, slates = lax.axis_size("seq"), lax.axis_size("slate")
    slate_items = float(item_rows * group)
    swap = lambda value: exchange(value, "seq", 1)
    normed, personal, (w_query, w_key, w_value) = prepare(user_ids, local_items, user_table, gain_in[None], [w_query, w_key, w_value])

    bits = list(range(2, group, 2))
    waves = [bits[i : i + 2] for i in range(0, len(bits), 2)]
    near = [exchange(normed, "seq", bit) for bit in waves[0]]
    partner = swap(normed)
    q_heads, w_value_t = project_queries(normed, w_query, w_value)
    (weighted,) = attend([normed, partner], w_key, w_value_t, q_heads)
    for i, wave in enumerate(waves):
        (near, normed), weighted = after((near, normed), weighted)
        partners = [swap(piece) for piece in near]
        following = [exchange(normed, "seq", bit) for bit in waves[i + 1]] if i + 1 < len(waves) else None
        (weighted,) = attend(near, w_key, w_value_t, q_heads, weighted)
        if following:
            (weighted,) = attend(partners, w_key, w_value_t, q_heads, weighted)
        near = following
    mixed, scored, sums = attend(
        partners,
        w_key,
        w_value_t,
        q_heads,
        weighted,
        [personal, local_items, w_out, gain_out[None], w_score[None], labels],
    )
    devices = group * slates
    sums = lax.all_to_all(jnp.broadcast_to(sums[:1], (devices, 128)), ("seq", "slate"), 0, 0, tiled=True)
    sums = jnp.sum(sums.reshape(group, slates, 128), axis=0)
    total_loss = jnp.sum(jnp.log(sums[:, 0] / slate_items) - sums[:, 2] / sums[:, 1])
    return (mixed[None], scored, total_loss)


def solution(mesh):
    return jax.shard_map(
        shards,
        mesh=mesh,
        in_specs=(
            P("slate", "seq", None),
            P("slate"),
            P("slate", "seq"),
            P(),
            P(),
            P(),
            P(),
            P(),
            P(),
            P(),
            P(),
        ),
        out_specs=(P("slate", "seq", None), P("slate", "seq"), P()),
        check_vma=False,
    )
```
